32 devices in a mesh: grp: 8 (over y, x, core), loc: 4 (over z).
Axes of the slice: x: 2, y: 2, z: 4, core: 2. Of those that a mesh axis runs over, the one named last changes fastest.
Arguments:
- element_values: float32 [8, 442368], P(None, ('grp', 'loc')), may hold values from -6 to 6
- local_map: int32 [442368], P(('grp', 'loc')), may hold values from 0 to 10647, as said below
- send_node: int32 [32, 3072], P(('grp', 'loc')), may hold values from 0 to 10647, as said below
- send_count: int32 [32, 12], P(('grp', 'loc')), may hold values from 0 to 256, as said below
- recv_slot: int32 [32, 3072], P(('grp', 'loc')), may hold values from 0 to 511, as said below
Outputs:
- summed: float32 [8, 442368], P(None, ('grp', 'loc'))
The draws below stay inside these ranges and needn't reach their ends.
Inputs may be any that keep to these rules, and one draw needn't show every extreme that they name: `local_map`: each device's block lists the nodes of its elements as points of a grid of 22 x 22 x 22 distinct nodes, elements in some order, the grid points numbered in an arbitrary order of the device's own; every number below 10648 appears in each block. `send_node`: the live slots toward one peer name distinct nodes; slots at or past a pair's count hold arbitrary node numbers. `send_count`: counts are zero toward groups past the ends of grp (no wrap), exactly 256 toward the device itself, and between 64 and 256 toward every other peer. `recv_slot`: the live slots from one sender to one owner name distinct owned nodes.
All inputs are finite; a program needn't handle non-finite values.
Results may differ from the reference program's by a relative error of at most 0.0003.
Values sent between devices are 32-bit elements; how exact they have to be, the bound alone decides.
A program may use at most 64 MiB of HBM per device.

```python
import jax
import jax.numpy as jnp
from jax import lax

FIELDS = 8
NODES = 512
EB = 3
ELEMS_DEV = 27
EDGE = 22
LOCAL = 10648
SLOTS = 256
OWNED = 512
ELEMS = 864
N_GRP = 8
N_LOC = 4
DEVICES = 32


def slot_counts(key):
    device = jnp.arange(DEVICES, dtype=jnp.int32)[:, None]
    peer = jnp.arange(3 * N_LOC, dtype=jnp.int32)[None, :]
    group = device // N_LOC
    place = device % N_LOC
    offset = peer // N_LOC - 1
    target = peer % N_LOC
    inside = (group + offset >= 0) & (group + offset < N_GRP)
    itself = (offset == 0) & (target == place)
    drawn = jax.random.randint(jax.random.fold_in(key, 21), (DEVICES, 3 * N_LOC), SLOTS // 4, SLOTS + 1)
    counted = jnp.where(itself, SLOTS, drawn)
    return jnp.where(inside, counted, 0).astype(jnp.int32)


def draw_send_count(key, part):
    return slot_counts(key)


def draw_send_node(key, part):
    counts = slot_counts(key)
    device_keys = jax.random.split(jax.random.fold_in(key, 12), DEVICES)
    orders = jax.vmap(lambda k: jax.random.permutation(k, LOCAL))(device_keys).astype(jnp.int32)
    starts = jax.random.randint(jax.random.fold_in(key, 16), (DEVICES, 3 * N_LOC), 0, LOCAL)
    spots = ((starts[:, :, None] + jnp.arange(SLOTS, dtype=jnp.int32)[None, None, :]) % LOCAL).reshape(DEVICES, 3 * N_LOC * SLOTS)
    chosen = jnp.take_along_axis(orders, spots.astype(jnp.int32), axis=1)
    filler = jax.random.randint(jax.random.fold_in(key, 13), (DEVICES, 3 * N_LOC * SLOTS), 0, LOCAL)
    live_slot = (jnp.arange(SLOTS)[None, None, :] < counts[:, :, None]).reshape(DEVICES, 3 * N_LOC * SLOTS)
    return jnp.where(live_slot, chosen, filler).astype(jnp.int32)


def draw_recv_slot(key, part):
    starts = jax.random.randint(jax.random.fold_in(key, 14), (DEVICES, 3 * N_LOC), 0, OWNED)
    slots_all = (starts[:, :, None] + jnp.arange(SLOTS, dtype=jnp.int32)[None, None, :]) % OWNED
    return slots_all.reshape(DEVICES, 3 * N_LOC * SLOTS).astype(jnp.int32)


def grid_table():
    element = jnp.arange(ELEMS_DEV, dtype=jnp.int32)[:, None]
    node = jnp.arange(NODES, dtype=jnp.int32)[None, :]
    first = 7 * (element // (EB * EB)) + node // 64
    second = 7 * (element // EB % EB) + node // 8 % 8
    third = 7 * (element % EB) + node % 8
    return ((first * EDGE + second) * EDGE + third).astype(jnp.int32)


def one_map(key):
    order = jax.random.permutation(jax.random.fold_in(key, 1), ELEMS_DEV)
    labels = jax.random.permutation(jax.random.fold_in(key, 2), LOCAL).astype(jnp.int32)
    return labels[grid_table()[order].reshape(-1)]


def draw_local_map(key, part):
    device_keys = jax.random.split(jax.random.fold_in(key, 15), DEVICES)
    return jax.vmap(one_map)(device_keys).reshape(-1).astype(jnp.int32)


def shard_levels(own_key, shape, cuts, least, top_value):
    gain, own = 1.0, jax.random.fold_in(own_key, 6)
    for dim, parts in cuts:
        steps = jnp.exp(jax.random.uniform(jax.random.fold_in(own, dim), (parts,), jnp.float32, least / len(cuts), top_value / len(cuts)))
        gain = gain * jnp.repeat(steps, shape[dim] // parts).reshape([-1 if axis == dim else 1 for axis in range(len(shape))])
    return gain


def bell_draw(rng, shape, width, limit, cuts=(), kind=jnp.bfloat16):
    entries = width * jax.random.normal(rng, shape, jnp.float32)
    if cuts:
        entries = entries * shard_levels(rng, shape, cuts, -0.22, 0.18)
    return jnp.clip(entries, -limit, limit).astype(kind)


def setup_inputs(seed: int = 0) -> dict:
    key_of = jax.random.split(jax.random.key(seed), 6)
    return {
        "element_values": bell_draw(key_of[0], (FIELDS, ELEMS * NODES), 1.0, 6.0, ((1, 32),), jnp.float32),
        "local_map": draw_local_map(jax.random.fold_in(key_of[5], 71), 0),
        "send_node": draw_send_node(jax.random.fold_in(key_of[5], 71), 0),
        "send_count": draw_send_count(jax.random.fold_in(key_of[5], 71), 0),
        "recv_slot": draw_recv_slot(jax.random.fold_in(key_of[5], 71), 0),
    }


def peer_ids(device, recv_slot):
    group = device // N_LOC
    place = device % N_LOC
    offset = jnp.arange(3, dtype=jnp.int32)[:, None, None]
    target_loc = jnp.arange(N_LOC, dtype=jnp.int32)[None, :, None]
    position = jnp.arange(SLOTS, dtype=jnp.int32)[None, None, :]
    owner = (jnp.clip(group + offset - 1, 0, N_GRP - 1) * N_LOC + target_loc).astype(jnp.int32)
    column = ((offset * N_LOC + place) * SLOTS + position).astype(jnp.int32)
    owner_b, column_b = jnp.broadcast_arrays(owner, column)
    slot_of = recv_slot[owner_b, column_b]
    return (owner_b * OWNED + slot_of).reshape(-1).astype(jnp.int32)


def reference(element_values, local_map, send_node, send_count, recv_slot):
    span = ELEMS_DEV * NODES

    def assemble(device):
        start = (device * span).astype(jnp.int32)
        block = lax.dynamic_slice_in_dim(element_values, start, span, 1)
        mapping = lax.dynamic_slice_in_dim(local_map, start, span, 0)
        assembled = jnp.zeros((FIELDS, LOCAL), jnp.float32).at[:, mapping].add(block)
        live_slot = (jnp.arange(SLOTS, dtype=jnp.int32)[None, :] < send_count[device][:, None]).reshape(-1)
        picked = jnp.where(live_slot[None, :], jnp.take(assembled, send_node[device], axis=1), jnp.float32(0.0))
        return assembled, mapping, live_slot, picked

    def add_device(totals, device):
        assembled, mapping, live_slot, picked = assemble(device)
        return totals.at[:, peer_ids(device, recv_slot)].add(picked), None

    devices = jnp.arange(DEVICES, dtype=jnp.int32)
    totals, _ = lax.scan(add_device, jnp.zeros((FIELDS, DEVICES * OWNED), jnp.float32), devices)

    def finish(device):
        assembled, mapping, live_slot, picked = assemble(device)
        back = jnp.take(totals, peer_ids(device, recv_slot), axis=1)
        change = jnp.where(live_slot[None, :], back - picked, jnp.float32(0.0))
        combined = assembled.at[:, send_node[device]].add(change)
        return jnp.take(combined, mapping, axis=1)

    spread = lax.map(finish, devices)
    return spread.transpose(1, 0, 2).reshape(FIELDS, DEVICES * span)
```

```python
import jax
import jax.numpy as jnp
from jax import lax
from jax.experimental import pallas as pl
from jax.experimental.pallas import tpu as pltpu
from jax.sharding import PartitionSpec as P

LOCAL = 10648


def shifted(block, axis, distance):
    devices = range(lax.axis_size(axis))
    route = [(i - distance, i) for i in devices if i - distance in devices]
    return lax.ppermute(block, axis, route)


def within_inward(buffer):
    return lax.all_to_all(buffer, "loc", split_axis=2, concat_axis=2, tiled=True)


def across_inward(buffer):
    lower = shifted(buffer[:, 0], "grp", -1)
    upper = shifted(buffer[:, 2], "grp", 1)
    return jnp.stack([lower, buffer[:, 1], upper], axis=1)


def within_outward(buffer):
    return lax.all_to_all(buffer, "loc", split_axis=2, concat_axis=2, tiled=True)


def across_outward(buffer):
    lower = shifted(buffer[:, 0], "grp", 1)
    upper = shifted(buffer[:, 2], "grp", -1)
    return jnp.stack([lower, buffer[:, 1], upper], axis=1)


BATCH = 32
ROWS = 10656


def add_rows(index_ref, value_ref, table_ref):
    def step(b, carry):
        base = pl.multiple_of(b * BATCH, BATCH)
        nodes = [index_ref[base + k] for k in range(BATCH)]
        held = [table_ref[pl.ds(n, 1), :] for n in nodes]
        sums = [held[k] + value_ref[pl.ds(base + k, 1), :] for k in range(BATCH)]
        for k in range(BATCH):
            table_ref[pl.ds(nodes[k], 1), :] = sums[k]
        return carry

    lax.fori_loop(0, index_ref.shape[0] // BATCH, step, 0)


def take_rows(index_ref, table_ref, out_ref):
    def step(b, carry):
        base = pl.multiple_of(b * BATCH, BATCH)
        rows = [table_ref[pl.ds(index_ref[base + k], 1), :] for k in range(BATCH)]
        for k in range(BATCH):
            out_ref[pl.ds(base + k, 1), :] = rows[k]
        return carry

    lax.fori_loop(0, index_ref.shape[0] // BATCH, step, 0)


def assemble_kernel(map_ref, send_ref, value_ref, table_ref, picked_ref):
    chunk = 288

    def clear(b, carry):
        table_ref[pl.ds(pl.multiple_of(b * chunk, chunk), chunk), :] = jnp.zeros((chunk, table_ref.shape[1]), jnp.float32)
        return carry

    lax.fori_loop(0, ROWS // chunk, clear, 0)
    add_rows(map_ref, value_ref, table_ref)
    take_rows(send_ref, table_ref, picked_ref)


def finish_kernel(map_ref, send_ref, change_ref, table_in, out_ref, table_ref):
    pltpu.sync_copy(table_in, table_ref)
    add_rows(send_ref, change_ref, table_ref)
    take_rows(map_ref, table_ref, out_ref)


SMEM = pl.BlockSpec(memory_space=pltpu.SMEM)
VMEM = pl.BlockSpec(memory_space=pltpu.VMEM)


def on_device(element_values, local_map, send_node, send_count, recv_slot):
    fields, span = element_values.shape
    loc_count = lax.axis_size("loc")
    slots_all = send_node.shape[1]
    slot_count = slots_all // (3 * loc_count)
    owned_count = 2 * slot_count
    params = pltpu.CompilerParams(vmem_limit_bytes=48 * 1024 * 1024)
    table, picked_rows = pl.pallas_call(
        assemble_kernel,
        out_shape=(
            jax.ShapeDtypeStruct((ROWS, fields), jnp.float32),
            jax.ShapeDtypeStruct((slots_all, fields), jnp.float32),
        ),
        in_specs=[SMEM, SMEM, VMEM],
        out_specs=(VMEM, VMEM),
        compiler_params=params,
    )(local_map, send_node[0], element_values.T)
    live_slot = (jnp.arange(slot_count)[None, :] < send_count[0][:, None]).reshape(-1)
    picked = jnp.where(live_slot[None, :], picked_rows.T, 0.0)
    outgoing = picked.reshape(fields, 3, loc_count, slot_count)
    arrived = within_inward(across_inward(outgoing))
    incoming = arrived.reshape(fields, -1)
    targets = recv_slot[0]
    totals = jnp.zeros((fields, owned_count), jnp.float32).at[:, targets].add(incoming, mode="promise_in_bounds")
    replies = totals.at[:, targets].get(mode="promise_in_bounds").reshape(fields, 3, loc_count, slot_count)
    homeward = across_outward(within_outward(replies))
    returned = homeward.reshape(fields, -1)
    change = jnp.where(live_slot[None, :], returned - picked, 0.0)
    spots = jnp.where(live_slot, send_node[0], LOCAL)
    summed = pl.pallas_call(
        finish_kernel,
        out_shape=jax.ShapeDtypeStruct((span, fields), jnp.float32),
        in_specs=[SMEM, SMEM, VMEM, pl.BlockSpec(memory_space=pl.ANY)],
        out_specs=VMEM,
        scratch_shapes=[pltpu.VMEM((ROWS, fields), jnp.float32)],
        compiler_params=params,
    )(local_map, spots, change.T, table)
    return summed.T


def solution(mesh):
    return jax.shard_map(
        on_device,
        mesh=mesh,
        in_specs=(
            P(None, ("grp", "loc")),
            P(("grp", "loc")),
            P(("grp", "loc"), None),
            P(("grp", "loc"), None),
            P(("grp", "loc"), None),
        ),
        out_specs=P(None, ("grp", "loc")),
        check_vma=False,
    )
```
